32 devices in a mesh: seq: 4 (over y, x), img: 2 (over core), dp: 4 (over z).
Axes of the slice: x: 2, y: 2, z: 4, core: 2. Of those that a mesh axis runs over, the one named last changes fastest.
Arguments:
- queries: bfloat16 [512, 8192], P('seq', 'dp'), may hold values from -22 to 22
- out_grad: bfloat16 [512, 8192], P('seq', 'dp'), may hold values from -600 to 600
- token_image: int32 [512], P('seq'), may hold values from -1 to 1, as said below
- unnormed_keys: bfloat16 [2, 6432, 1024], P('img', 'seq', 'dp'), may hold values from -14 to 14
- values: bfloat16 [2, 6432, 1024], P('img', 'seq', 'dp'), may hold values from -6 to 6
- key_gain: float32 [128], replicated, may hold values from 0.1 to 1.9
- tile_count: int32 [2], replicated, may hold values from 1 to 4, as said below
- key_projection_matrix: bfloat16 [8192, 1024], P('dp', 'seq'), may hold values from -0.1875 to 0.1875
- value_projection_matrix: bfloat16 [8192, 1024], P('dp', 'seq'), may hold values from -0.1875 to 0.1875
Outputs:
- feature_grad: bfloat16 [2, 6432, 8192], P('img', 'seq', 'dp')
The draws below stay inside these ranges and needn't reach their ends.
Inputs may be any that keep to these rules, and one draw needn't show every extreme that they name: `token_image`: in each block of 128 tokens (one index of seq) at most 16 tokens name one image, and some image is named by exactly 16; -1 marks a token that attends no image. `tile_count`: some image has 4 tiles.
All inputs are finite; a program needn't handle non-finite values.
Results may differ from the reference program's by a relative error of at most 0.0067.
Values may be sent and summed in bfloat16 or wider, within the bound.
A program may use at most 128 MiB of HBM per device.

```python
import jax
import jax.numpy as jnp
from jax import lax

MODEL_WIDTH = 8192
QUERY_HEAD_COUNT = 64
KEY_VALUE_HEADS = 8
HEAD_WIDTH = 128
TILES = 4
TILE_TOK = 1601
TILE_ROWS = 1608
IMAGE_ROW_COUNT = 6432
TOK_DEV = 128
CAP = 16
IMAGE_COUNT = 2
TEXT_TOKENS = 512
N_SEQ = 4


def image_ids(key):
    random_key_seed = jax.random.fold_in(key, 11)
    blocks = TEXT_TOKENS // TOK_DEV
    group_count = TOK_DEV // CAP
    block_keys = jax.random.split(jax.random.fold_in(random_key_seed, 1), blocks)

    def block_perm(block_key):
        return jax.random.permutation(block_key, IMAGE_COUNT)
    image_perm = jax.vmap(block_perm)(block_keys)
    group_fill = jax.random.randint(jax.random.fold_in(random_key_seed, 2), (blocks, group_count), CAP * 3 // 4, CAP + 1)
    group_fill = jnp.where(jnp.arange(group_count)[None, :] == 0, CAP, group_fill)
    position = jnp.arange(TOK_DEV)
    group_id = position // CAP
    offset = position % CAP
    chosen = image_perm[:, jnp.minimum(group_id, IMAGE_COUNT - 1)]
    is_kept = (group_id[None, :] < IMAGE_COUNT) & (offset[None, :] < group_fill[:, group_id])
    return jnp.where(is_kept, chosen, -1).reshape(TEXT_TOKENS).astype(jnp.int32)


def base_keys(key):
    random_key_seed = jax.random.fold_in(key, 17)
    array_shape = (IMAGE_COUNT, IMAGE_ROW_COUNT, KEY_VALUE_HEADS * HEAD_WIDTH)
    raw_keys = jnp.clip(jax.random.normal(jax.random.fold_in(random_key_seed, 4), array_shape), -6.0, 6.0)
    return raw_keys.astype(jnp.float32)


def draw_token_image(key, part):
    return image_ids(key)


def draw_unnormed_keys(key, part):
    return base_keys(key).astype(jnp.bfloat16)


def draw_tile_count(key, part):
    random_key_seed = jax.random.fold_in(key, 23)
    counts = jax.random.randint(jax.random.fold_in(random_key_seed, 1), (IMAGE_COUNT,), 1, TILES + 1)
    full_image = jax.random.randint(jax.random.fold_in(random_key_seed, 2), (), 0, IMAGE_COUNT)
    image_axis = jnp.arange(IMAGE_COUNT)
    counts = jnp.where(image_axis == full_image, TILES, counts)
    return counts.astype(jnp.int32)


def draw_queries(key, part):
    random_key_seed = jax.random.fold_in(key, 19)
    array_shape = (TEXT_TOKENS, QUERY_HEAD_COUNT * HEAD_WIDTH)
    query_values = jnp.clip(jax.random.normal(jax.random.fold_in(random_key_seed, 5), array_shape), -6.0, 6.0)
    return query_values.astype(jnp.float32).astype(jnp.bfloat16)


def level_of(own_key, dims, shards, low, high):
    def one(dim, parts):
        heights = jax.random.uniform(jax.random.fold_in(jax.random.fold_in(own_key, 6), dim), (parts,), jnp.float32, low / len(shards), high / len(shards))
        return jnp.repeat(jnp.exp(heights), dims[dim] // parts).reshape((-1,) + (1,) * (len(dims) - dim - 1))

    gain = one(*shards[0])
    for cut in shards[1:]:
        gain = gain * one(*cut)
    return gain


def centred(key, dims, spread, bound, shards=(), held_as=jnp.bfloat16):
    gain = level_of(key, dims, shards, -0.22, 0.18) if shards else 1.0
    array = jax.random.normal(key, dims, jnp.float32) * spread * gain
    return jnp.minimum(jnp.maximum(array, -bound), bound).astype(held_as)


def setup_inputs(seed: int = 0) -> dict:
    seeds = jax.random.split(jax.random.key(seed), 10)
    queries = draw_queries(jax.random.fold_in(seeds[9], 71), 0)
    out_grad = centred(seeds[1], (TEXT_TOKENS, QUERY_HEAD_COUNT * HEAD_WIDTH), 100.0, 600.0, ((0, 4), (1, 4)))
    token_image = draw_token_image(jax.random.fold_in(seeds[9], 71), 0)
    unnormed_keys = draw_unnormed_keys(jax.random.fold_in(seeds[9], 71), 0)
    values = centred(seeds[4], (IMAGE_COUNT, IMAGE_ROW_COUNT, KEY_VALUE_HEADS * HEAD_WIDTH), 1.0, 6.0, ((0, 2), (1, 4), (2, 4)))
    key_gain = jnp.clip(1.0 + 0.18 * jax.random.normal(seeds[5], (HEAD_WIDTH,), jnp.float32), 0.1, 1.9)
    tile_count = draw_tile_count(jax.random.fold_in(seeds[9], 71), 0)
    key_projection_matrix = centred(seeds[7], (MODEL_WIDTH, KEY_VALUE_HEADS * HEAD_WIDTH), (KEY_VALUE_HEADS * HEAD_WIDTH) ** -0.5, 0.1875, ((0, 4), (1, 4)))
    value_projection_matrix = centred(seeds[8], (MODEL_WIDTH, KEY_VALUE_HEADS * HEAD_WIDTH), (KEY_VALUE_HEADS * HEAD_WIDTH) ** -0.5, 0.1875, ((0, 4), (1, 4)))
    return dict(queries=queries, out_grad=out_grad, token_image=token_image, unnormed_keys=unnormed_keys, values=values, key_gain=key_gain, tile_count=tile_count, key_projection_matrix=key_projection_matrix, value_projection_matrix=value_projection_matrix)


epsilon = 1e-05
masked = -1e+30

def reference(queries, out_grad, token_image, unnormed_keys, values, key_gain, tile_count, key_projection_matrix, value_projection_matrix):
    group_length = QUERY_HEAD_COUNT // KEY_VALUE_HEADS
    score_scale = HEAD_WIDTH ** (-0.5)
    text_rows = N_SEQ * CAP
    row_ids = jnp.arange(IMAGE_ROW_COUNT, dtype=jnp.int32)
    token_ids = jnp.arange(TEXT_TOKENS, dtype=jnp.int32)
    gain_float = key_gain.astype(jnp.float32)
    contracting = (((1,), (1,)), ((), ()))
    leading = (((0,), (0,)), ((), ()))

    def per_image(image_number):
        attends = token_image == image_number
        text_order = jnp.argsort(jnp.where(attends, token_ids, token_ids + TEXT_TOKENS))[:text_rows].astype(jnp.int32)
        is_valid = attends[text_order][:, None]
        text_query = jnp.where(is_valid, queries[text_order], jnp.zeros((), jnp.bfloat16))
        text_grad = jnp.where(is_valid, out_grad[text_order], jnp.zeros((), jnp.bfloat16))
        unnormed_float = lax.dynamic_index_in_dim(unnormed_keys, image_number, 0, keepdims=False).astype(jnp.float32).reshape(IMAGE_ROW_COUNT, KEY_VALUE_HEADS, HEAD_WIDTH)
        value_row_block = lax.dynamic_index_in_dim(values, image_number, 0, keepdims=False).reshape(IMAGE_ROW_COUNT, KEY_VALUE_HEADS, HEAD_WIDTH)
        inverse = lax.rsqrt(lax.optimization_barrier(jnp.mean(unnormed_float * unnormed_float, axis=-1, keepdims=True)) + epsilon)
        unit_key = unnormed_float * inverse
        normed = (unit_key * gain_float).astype(jnp.bfloat16)
        tile_limit = jnp.sum(jnp.where(jnp.arange(IMAGE_COUNT, dtype=jnp.int32) == image_number, tile_count, 0))
        live_rows = (row_ids // TILE_ROWS < tile_limit) & (row_ids % TILE_ROWS < TILE_TOK)

        def per_head(head_index):
            kv_head = head_index // group_length
            query_head = lax.dynamic_slice_in_dim(text_query, head_index * HEAD_WIDTH, HEAD_WIDTH, 1)
            grad_head = lax.dynamic_slice_in_dim(text_grad, head_index * HEAD_WIDTH, HEAD_WIDTH, 1)
            key_head = lax.dynamic_index_in_dim(normed, kv_head, 1, keepdims=False)
            value_head = lax.dynamic_index_in_dim(value_row_block, kv_head, 1, keepdims=False)
            scores = lax.dot_general(query_head, key_head, contracting, preferred_element_type=jnp.float32) * score_scale
            scores = jnp.where(live_rows[None, :], scores, masked)
            row_top = lax.optimization_barrier(jnp.max(scores, axis=-1, keepdims=True))
            exponent = jnp.exp(scores - row_top)
            probabilities = exponent / lax.optimization_barrier(jnp.sum(exponent, axis=-1, keepdims=True))
            grad_probs = lax.dot_general(grad_head, value_head, contracting, preferred_element_type=jnp.float32)
            inner_sum = lax.optimization_barrier(jnp.sum(probabilities * grad_probs, axis=-1, keepdims=True))
            probs_low = probabilities.astype(jnp.bfloat16)
            score_grad = (probabilities * (grad_probs - inner_sum)).astype(jnp.bfloat16)
            value_part = lax.dot_general(probs_low, grad_head, leading, preferred_element_type=jnp.float32)
            key_part = lax.dot_general(score_grad, query_head, leading, preferred_element_type=jnp.float32) * score_scale
            return (key_part, value_part)
        key_pieces_list, value_pieces_list = lax.map(per_head, jnp.arange(QUERY_HEAD_COUNT, dtype=jnp.int32))
        normalized_gradient = jnp.transpose(key_pieces_list.reshape(KEY_VALUE_HEADS, group_length, IMAGE_ROW_COUNT, HEAD_WIDTH).sum(axis=1), (1, 0, 2))
        value_gradient = jnp.transpose(value_pieces_list.reshape(KEY_VALUE_HEADS, group_length, IMAGE_ROW_COUNT, HEAD_WIDTH).sum(axis=1), (1, 0, 2))
        unit_grad = normalized_gradient * gain_float
        key_gradient = inverse * (unit_grad - unit_key * lax.optimization_barrier(jnp.mean(unit_grad * unit_key, axis=-1, keepdims=True)))
        key_reduced_precision = key_gradient.astype(jnp.bfloat16).reshape(IMAGE_ROW_COUNT, KEY_VALUE_HEADS * HEAD_WIDTH)
        value_reduced_precision = value_gradient.astype(jnp.bfloat16).reshape(IMAGE_ROW_COUNT, KEY_VALUE_HEADS * HEAD_WIDTH)
        feature_out = lax.dot_general(key_reduced_precision, key_projection_matrix, contracting, preferred_element_type=jnp.float32)
        feature_out = feature_out + lax.dot_general(value_reduced_precision, value_projection_matrix, contracting, preferred_element_type=jnp.float32)
        return feature_out.astype(jnp.bfloat16)
    return lax.map(per_image, jnp.arange(IMAGE_COUNT, dtype=jnp.int32))
```

```python
import functools

import jax
import jax.numpy as jnp
from jax import lax
from jax.experimental import pallas as pl
from jax.experimental.pallas import tpu as pltpu
from jax.sharding import PartitionSpec as P

QUERY_HEAD_COUNT = 64
KEY_VALUE_HEADS = 8
HEAD_WIDTH = 128
TILE_TOK = 1601
TILE_ROWS = 1608
CAP = 16


epsilon = 1e-05
masked = -1e30


def body_any(
    queries,
    out_grad,
    token_image,
    unnormed_keys,
    values,
    key_gain,
    tile_count,
    key_projection_matrix,
    value_projection_matrix,
):
    image_number = lax.axis_index("img")
    seq_index = lax.axis_index("seq")
    attends = token_image == image_number
    slot_rank = jnp.cumsum(attends.astype(jnp.int32)) - 1
    picker = (
        attends[None, :] & (slot_rank[None, :] == jnp.arange(CAP, dtype=jnp.int32)[:, None])
    ).astype(jnp.bfloat16)
    packed_query = jnp.dot(picker, queries, preferred_element_type=jnp.float32).astype(jnp.bfloat16)
    packed_grad = jnp.dot(picker, out_grad, preferred_element_type=jnp.float32).astype(jnp.bfloat16)
    text_query, text_grad = (
        lax.all_gather(packed_query, "seq", axis=0, tiled=True),
        lax.all_gather(packed_grad, "seq", axis=0, tiled=True),
    )
    key_rows = unnormed_keys.shape[1]
    key_width = unnormed_keys.shape[2]
    key_heads = key_width // HEAD_WIDTH
    group_length = QUERY_HEAD_COUNT // KEY_VALUE_HEADS
    text_rows = text_query.shape[0]
    score_scale = HEAD_WIDTH ** (-0.5)
    unnormed_float = unnormed_keys[0].astype(jnp.float32).reshape(key_rows, key_heads, HEAD_WIDTH)
    inverse = lax.rsqrt(jnp.mean(unnormed_float * unnormed_float, axis=-1, keepdims=True) + epsilon)
    unit_key = unnormed_float * inverse
    normed = (unit_key * key_gain).astype(jnp.bfloat16)
    value_heads = values[0].reshape(key_rows, key_heads, HEAD_WIDTH)
    query_heads = text_query.reshape(text_rows, key_heads, group_length, HEAD_WIDTH)
    grad_heads = text_grad.reshape(text_rows, key_heads, group_length, HEAD_WIDTH)
    row_global = seq_index * key_rows + jnp.arange(key_rows, dtype=jnp.int32)
    tile_limit = jnp.sum(
        jnp.where(jnp.arange(tile_count.shape[0], dtype=jnp.int32) == image_number, tile_count, 0)
    )
    live_rows = (row_global // TILE_ROWS < tile_limit) & (row_global % TILE_ROWS < TILE_TOK)
    scores = (
        jnp.einsum("rhge,khe->hgrk", query_heads, normed, preferred_element_type=jnp.float32)
        * score_scale
    )
    scores = jnp.where(live_rows, scores, masked)
    grad_probs = jnp.einsum(
        "rhge,khe->hgrk", grad_heads, value_heads, preferred_element_type=jnp.float32
    )
    row_top = lax.pmax(jnp.max(scores, axis=-1), "seq")
    exponent = jnp.exp(scores - row_top[..., None])
    row_total = lax.psum(jnp.sum(exponent, axis=-1), "seq")
    probabilities = exponent / row_total[..., None]
    inner_sum = lax.psum(jnp.sum(probabilities * grad_probs, axis=-1), "seq")
    probs_low = probabilities.astype(jnp.bfloat16)
    score_grad = (probabilities * (grad_probs - inner_sum[..., None])).astype(jnp.bfloat16)
    value_gradient = jnp.einsum(
        "hgrk,rhge->khe", probs_low, grad_heads, preferred_element_type=jnp.float32
    )
    normalized_gradient = (
        jnp.einsum("hgrk,rhge->khe", score_grad, query_heads, preferred_element_type=jnp.float32)
        * score_scale
    )
    unit_grad = normalized_gradient * key_gain
    key_gradient = inverse * (
        unit_grad - unit_key * jnp.mean(unit_grad * unit_key, axis=-1, keepdims=True)
    )
    key_reduced_precision = key_gradient.astype(jnp.bfloat16).reshape(key_rows, key_width)
    value_reduced_precision = value_gradient.astype(jnp.bfloat16).reshape(key_rows, key_width)
    key_all, value_all = (
        lax.all_gather(key_reduced_precision, "dp", axis=1, tiled=True),
        lax.all_gather(value_reduced_precision, "dp", axis=1, tiled=True),
    )
    contracting = (((1,), (1,)), ((), ()))
    partial_value = lax.dot_general(
        key_all,
        lax.all_gather(key_projection_matrix, "seq", axis=1, tiled=True),
        contracting,
        preferred_element_type=jnp.float32,
    )
    feature_sum = partial_value + lax.dot_general(
        value_all,
        lax.all_gather(value_projection_matrix, "seq", axis=1, tiled=True),
        contracting,
        preferred_element_type=jnp.float32,
    )
    return feature_sum.astype(jnp.bfloat16)[None]


MESH = pl.DeviceIdType.MESH
NT = (((1,), (1,)), ((), ()))
NN = (((1,), (0,)), ((), ()))
CHUNK = 272
FEATURE_TILE = 256
VMEM_BYTES = 67043328


def dot(a, b, dims):
    return lax.dot_general(a, b, dims, preferred_element_type=jnp.float32)


def kernel(
    sizes,
    image_ref,
    limit_ref,
    query_hbm,
    grad_hbm,
    key_hbm,
    value_hbm,
    gain_ref,
    key_weight_ref,
    value_weight_ref,
    out_ref,
    query_ref,
    grad_ref,
    key_ref,
    value_ref,
    normed_ref,
    raw,
    partial,
    text,
    score,
    grad_prob,
    stats,
    outer_stats,
    rows_all,
    weights,
    load_sem,
    text_send,
    text_recv,
    stat_send,
    stat_recv,
    weight_local,
    weight_send,
    weight_recv,
    relay_send,
    relay_recv,
    row_send,
    row_recv,
    raw_send,
    raw_recv,
):
    n_seq, n_dp, heads, group = sizes
    seq = lax.axis_index("seq")
    img = lax.axis_index("img")
    dp = lax.axis_index("dp")
    rows, width = key_ref.shape
    features = key_weight_ref.shape[0]
    half = features // 2
    stack = group * CAP
    query_rows = n_seq * stack
    full = rows // CHUNK
    rest = rows - full * CHUNK
    chunks = [(c * CHUNK, CHUNK) for c in range(full)] + [(full * CHUNK, rest)]
    scale = HEAD_WIDTH ** (-0.5)
    near, far = seq % 2, seq // 2
    seq_peers = [far * 2 + 1 - near, (1 - far) * 2 + near, (1 - far) * 2 + 1 - near]
    step = 1 - 2 * (dp // 2)
    inner, outer, second = dp + step, dp - step, dp + 2 * step
    farthest = (n_dp - 1) * (1 - dp // 2)
    is_end = (dp == 0) | (dp == n_dp - 1)
    is_middle = (dp > 0) & (dp < n_dp - 1)
    extra = heads

    loads = [
        pltpu.make_async_copy(source, target, load_sem.at[k])
        for k, (source, target) in enumerate(
            (
                (query_hbm, query_ref),
                (grad_hbm, grad_ref),
                (key_hbm, key_ref),
                (value_hbm, value_ref),
            )
        )
    ]
    for copy in loads:
        copy.start()

    barrier = pltpu.get_barrier_semaphore()
    for peer in seq_peers:
        pl.semaphore_signal(barrier, inc=1, device_id={"seq": peer}, device_id_type=MESH)
    pl.semaphore_signal(barrier, inc=1, device_id={"img": 1 - img}, device_id_type=MESH)
    pl.semaphore_signal(barrier, inc=1, device_id={"dp": inner}, device_id_type=MESH)

    @pl.when(is_middle)
    def _():
        pl.semaphore_signal(barrier, inc=1, device_id={"dp": outer}, device_id_type=MESH)

    own_weights = [
        pltpu.make_async_copy(
            ref.at[:, pl.ds(h * HEAD_WIDTH, HEAD_WIDTH)],
            weights.at[seq, :, pl.ds((2 * h + k) * HEAD_WIDTH, HEAD_WIDTH)],
            weight_local.at[k, h],
        )
        for k, ref in enumerate((key_weight_ref, value_weight_ref))
        for h in range(heads)
    ]
    for copy in own_weights:
        copy.start()

    tokens = image_ref.shape[1]
    attends = image_ref[...] == img
    upper = (
        lax.broadcasted_iota(jnp.int32, (tokens, tokens), 0)
        <= lax.broadcasted_iota(jnp.int32, (tokens, tokens), 1)
    ).astype(jnp.bfloat16)
    counts = dot(
        jnp.broadcast_to(attends.astype(jnp.float32), (CAP, tokens)).astype(jnp.bfloat16), upper, NN
    )
    slot = lax.broadcasted_iota(jnp.int32, (CAP, tokens), 0).astype(jnp.float32) + 1.0
    picker = jnp.where(attends & (counts == slot), 1.0, 0.0).astype(jnp.bfloat16)

    def raw_copy(k):
        source = (key_hbm, value_hbm)[k]
        return pltpu.make_async_remote_copy(
            src_ref=source.at[:, pl.ds(HEAD_WIDTH, HEAD_WIDTH)],
            dst_ref=raw.at[k],
            send_sem=raw_send.at[k],
            recv_sem=raw_recv.at[k],
            device_id={"dp": outer},
            device_id_type=MESH,
        )

    def text_outer():
        return pltpu.make_async_remote_copy(
            src_ref=text.at[seq, heads - 1],
            dst_ref=text.at[seq, extra],
            send_sem=raw_send.at[2],
            recv_sem=text_recv.at[extra, seq],
            device_id={"dp": outer},
            device_id_type=MESH,
        )

    def stat_outer():
        return pltpu.make_async_remote_copy(
            src_ref=outer_stats.at[0],
            dst_ref=outer_stats.at[1],
            send_sem=raw_send.at[3],
            recv_sem=raw_recv.at[2],
            device_id={"dp": outer},
            device_id_type=MESH,
        )

    def text_copy(h, owner, peer, j):
        return pltpu.make_async_remote_copy(
            src_ref=text.at[owner, h],
            dst_ref=text.at[owner, h],
            send_sem=text_send.at[h, j],
            recv_sem=text_recv.at[h, owner],
            device_id={"seq": peer},
            device_id_type=MESH,
        )

    pl.semaphore_wait(barrier, n_seq - 1 + 1 + 1 + is_middle.astype(jnp.int32))

    @pl.when(is_middle)
    def _():
        raw_copy(0).start()

    for copy in loads[:2]:
        copy.wait()
    for h in range(heads):
        for k, ref in enumerate((query_ref, grad_ref)):
            first = h * group * HEAD_WIDTH
            packed = dot(picker, ref[:, first : first + group * HEAD_WIDTH], NN).astype(jnp.bfloat16)
            for g in range(group):
                column = g * HEAD_WIDTH
                text[seq, h, k, g * CAP : (g + 1) * CAP, :] = packed[:, column : column + HEAD_WIDTH]
        for j, peer in enumerate(seq_peers):
            text_copy(h, seq, peer, j).start()

    @pl.when(is_middle)
    def _():
        text_outer().start()
        raw_copy(1).start()

    gain = gain_ref[...]
    live_limit = limit_ref[img]

    def unit_of(k):
        inverse = lax.rsqrt(jnp.mean(k * k, axis=-1, keepdims=True) + epsilon)
        return k * inverse, inverse

    def own_key(row0, size, h):
        return key_ref[pl.ds(row0, size), h * HEAD_WIDTH : (h + 1) * HEAD_WIDTH].astype(jnp.float32)

    def text_of(h, k):
        return text[:, h, k].reshape(query_rows, HEAD_WIDTH)

    def live_of(row0, size):
        row = seq * rows + row0 + lax.broadcasted_iota(jnp.int32, (size, 1), 0)
        return (row // TILE_ROWS < live_limit) & (row % TILE_ROWS < TILE_TOK)

    def over_chunks(act, carry):
        carry = lax.fori_loop(
            0, full, lambda i, c: act(pl.multiple_of(i * CHUNK, 16), CHUNK, c), carry
        )
        return act(full * CHUNK, rest, carry)

    for copy in loads[2:]:
        copy.wait()

    def normalize_chunk(row0, size, carry):
        for h in range(heads):
            unit, _ = unit_of(own_key(row0, size, h))
            normed_ref[pl.ds(row0, size), h * HEAD_WIDTH : (h + 1) * HEAD_WIDTH] = (
                unit * gain
            ).astype(jnp.bfloat16)
        return carry

    over_chunks(normalize_chunk, 0)

    def stat_copy(h, owner, peer, j):
        return pltpu.make_async_remote_copy(
            src_ref=stats.at[owner, h],
            dst_ref=stats.at[owner, h],
            send_sem=stat_send.at[h, j],
            recv_sem=stat_recv.at[h, owner],
            device_id={"seq": peer},
            device_id_type=MESH,
        )

    for h in range(heads):
        lanes = slice(h * HEAD_WIDTH, (h + 1) * HEAD_WIDTH)
        for j, owner in enumerate(seq_peers):
            text_copy(h, owner, owner, j).wait_recv()

        def first_pass(row0, size, top):
            s = dot(normed_ref[pl.ds(row0, size), lanes], text_of(h, 0), NT) * scale
            s = jnp.where(live_of(row0, size), s, masked)
            score[h, pl.ds(row0, size), :] = s
            return jnp.maximum(top, jnp.max(s, axis=0, keepdims=True))

        top = over_chunks(first_pass, jnp.full((1, query_rows), masked, jnp.float32))

        def second_pass(row0, size, sums):
            e = jnp.exp(score[h, pl.ds(row0, size), :] - top)
            p = dot(value_ref[pl.ds(row0, size), lanes], text_of(h, 1), NT)
            score[h, pl.ds(row0, size), :] = e
            grad_prob[h, pl.ds(row0, size), :] = p
            return (
                sums[0] + jnp.sum(e, axis=0, keepdims=True),
                sums[1] + jnp.sum(e * p, axis=0, keepdims=True),
            )

        sums = over_chunks(
            second_pass, tuple(jnp.zeros((1, query_rows), jnp.float32) for _ in range(2))
        )
        stats[seq, h, 0:1, :] = top
        stats[seq, h, 1:2, :] = sums[0]
        stats[seq, h, 2:3, :] = sums[1]
        stats[seq, h, 3:8, :] = jnp.zeros((5, query_rows), jnp.float32)
        for j, peer in enumerate(seq_peers):
            stat_copy(h, seq, peer, j).start()

    @pl.when(is_end)
    def _():
        text_outer().wait_recv()
        for j, peer in enumerate(seq_peers):
            text_copy(extra, seq, peer, j).start()

    def weight_copy(owner, peer, j):
        part = weights.at[owner, pl.ds(pl.multiple_of(img * half, half), half)]
        return pltpu.make_async_remote_copy(
            src_ref=part,
            dst_ref=part,
            send_sem=weight_send.at[j],
            recv_sem=weight_recv.at[owner],
            device_id={"seq": peer},
            device_id_type=MESH,
        )

    def relay_copy(owner, j, which):
        part = weights.at[owner, pl.ds(pl.multiple_of(which * half, half), half)]
        return pltpu.make_async_remote_copy(
            src_ref=part,
            dst_ref=part,
            send_sem=relay_send.at[j],
            recv_sem=relay_recv.at[owner],
            device_id={"img": 1 - img},
            device_id_type=MESH,
        )

    for copy in own_weights:
        copy.wait()
    for j, peer in enumerate(seq_peers):
        weight_copy(seq, peer, j).start()

    def combine(h):
        for j, peer in enumerate(seq_peers):
            stat_copy(h, peer, peer, j).wait_recv()
        tops = [stats[i, h, 0:1, :] for i in range(n_seq)]
        top = functools.reduce(jnp.maximum, tops)
        factors = [jnp.exp(t - top) for t in tops]
        total = sum(f * stats[i, h, 1:2, :] for i, f in enumerate(factors))
        inner_sum = sum(f * stats[i, h, 2:3, :] for i, f in enumerate(factors)) / total
        own = jnp.exp(stats[seq, h, 0:1, :] - top) / total
        return top, 1.0 / total, inner_sum, own

    def row_copy(kind, owner, h, c, row0, size, peer):
        lane0, lanes = (0, 2 * width) if h is None else (2 * h * HEAD_WIDTH, 2 * HEAD_WIDTH)
        part = rows_all.at[owner, pl.ds(row0, size), pl.ds(lane0, lanes)]
        return pltpu.make_async_remote_copy(
            src_ref=part,
            dst_ref=part,
            send_sem=row_send.at[kind, c],
            recv_sem=row_recv.at[owner, 0 if h == 0 else 1, c],
            device_id={"dp": peer},
            device_id_type=MESH,
        )

    def arrive(owner, h, c, row0, size):
        row_copy(0, owner, h, c, row0, size, inner).wait_recv()

    def own_inner(h, c, row0, size):
        return row_copy(h, dp, h, c, row0, size, inner)

    def own_outer(c, row0, size):
        return row_copy(2, dp, 0, c, row0, size, outer)

    def inner_outer(h, c, row0, size):
        return row_copy(3 + h, inner, h, c, row0, size, outer)

    def far_outer(c, row0, size):
        return row_copy(5, farthest, None, c, row0, size, outer)

    def outer_inner(c, row0, size):
        return row_copy(6, outer, None, c, row0, size, inner)

    def finish(owner, h, which, row0, size, p, g, unit, inverse):
        value_gradient = dot(p.astype(jnp.bfloat16), text_of(which, 1), NN)
        unit_grad = dot(g.astype(jnp.bfloat16), text_of(which, 0), NN) * scale * gain
        key_gradient = inverse * (
            unit_grad - unit * jnp.mean(unit_grad * unit, axis=-1, keepdims=True)
        )
        lane = 2 * h * HEAD_WIDTH
        rows_all[owner, pl.ds(row0, size), lane : lane + HEAD_WIDTH] = key_gradient.astype(
            jnp.bfloat16
        )
        lane = lane + HEAD_WIDTH
        rows_all[owner, pl.ds(row0, size), lane : lane + HEAD_WIDTH] = value_gradient.astype(
            jnp.bfloat16
        )

    for h in range(heads):
        top, inverse_total, inner_sum, own_factor = combine(h)
        if h == heads - 1:
            outer_stats[0, 0:1, :] = top
            outer_stats[0, 1:2, :] = inverse_total
            outer_stats[0, 2:3, :] = inner_sum
            outer_stats[0, 3:8, :] = jnp.zeros((5, query_rows), jnp.float32)

            @pl.when(is_middle)
            def _():
                stat_outer().start()

        def own_pass(c, row0, size):
            p = score[h, pl.ds(row0, size), :] * own_factor
            g = p * (grad_prob[h, pl.ds(row0, size), :] - inner_sum)
            finish(dp, h, h, row0, size, p, g, *unit_of(own_key(row0, size, h)))
            own_inner(h, c, row0, size).start()
            if h == 0:

                @pl.when(is_middle)
                def _():
                    own_outer(c, row0, size).start()

        def own_chunk(i, _):
            own_pass(i, pl.multiple_of(i * CHUNK, 16), CHUNK)
            return 0

        lax.fori_loop(0, full, own_chunk, 0)
        own_pass(full, full * CHUNK, rest)

    @pl.when(is_middle)
    def _():
        for c, (row0, size) in enumerate(chunks):
            arrive(outer, 0, c, row0, size)
            arrive(inner, 0, c, row0, size)
            inner_outer(0, c, row0, size).start()
        for c, (row0, size) in enumerate(chunks):
            arrive(inner, 1, c, row0, size)
            inner_outer(1, c, row0, size).start()
            arrive(outer, 1, c, row0, size)
            outer_inner(c, row0, size).start()

    @pl.when(is_end)
    def _():
        for j, owner in enumerate(seq_peers):
            text_copy(extra, owner, owner, j).wait_recv()
        for k in range(2):
            raw_copy(k).wait_recv()
        stat_outer().wait_recv()
        top = outer_stats[1, 0:1, :]
        inverse_total = outer_stats[1, 1:2, :]
        inner_sum = outer_stats[1, 2:3, :]

        def extra_pass(row0, size, carry):
            unit, inverse = unit_of(raw[0, pl.ds(row0, size), :].astype(jnp.float32))
            s = dot((unit * gain).astype(jnp.bfloat16), text_of(extra, 0), NT) * scale
            s = jnp.where(live_of(row0, size), s, masked)
            p = jnp.exp(s - top) * inverse_total
            g = p * (dot(raw[1, pl.ds(row0, size), :], text_of(extra, 1), NT) - inner_sum)
            finish(inner, heads - 1, extra, row0, size, p, g, unit, inverse)
            return carry

        over_chunks(extra_pass, 0)

    for j, peer in enumerate(seq_peers):
        weight_copy(peer, peer, j).wait_recv()
        relay_copy(peer, j, img).start()

    @pl.when(is_end)
    def _():
        for c, (row0, size) in enumerate(chunks):
            arrive(inner, 0, c, row0, size)
        for h in range(heads):
            for c, (row0, size) in enumerate(chunks):
                arrive(second, h, c, row0, size)

    for j, peer in enumerate(seq_peers):
        relay_copy(peer, j, 1 - img).wait_recv()

    def last_product(block, column):
        return dot(
            rows_all[block, full * CHUNK : rows, :],
            weights[block, pl.ds(column, FEATURE_TILE), :],
            NT,
        )

    def partial_tile(i, _):
        column = pl.multiple_of(i * FEATURE_TILE, FEATURE_TILE)
        partial[:, pl.ds(column, FEATURE_TILE)] = functools.reduce(
            jnp.add, [last_product(dp // 2 + b, column) for b in range(n_dp - 1)]
        )
        return 0

    def last_tile(i, _):
        column = pl.multiple_of(i * FEATURE_TILE, FEATURE_TILE)
        total = partial[:, pl.ds(column, FEATURE_TILE)] + last_product(farthest, column)
        out_ref[full * CHUNK : rows, pl.ds(column, FEATURE_TILE)] = total.astype(out_ref.dtype)
        return 0

    def multiply(row0, size):
        def tile(i, _):
            column = pl.multiple_of(i * FEATURE_TILE, FEATURE_TILE)
            total = functools.reduce(
                jnp.add,
                [
                    dot(
                        rows_all[b, pl.ds(row0, size), :],
                        weights[b, pl.ds(column, FEATURE_TILE), :],
                        NT,
                    )
                    for b in range(n_dp)
                ],
            )
            out_ref[pl.ds(row0, size), pl.ds(column, FEATURE_TILE)] = total.astype(out_ref.dtype)
            return 0

        lax.fori_loop(0, features // FEATURE_TILE, tile, 0)

    def last_arrival(c, row0, size):
        arrive(farthest, None, c, row0, size)

        @pl.when(is_middle)
        def _():
            far_outer(c, row0, size).start()

    def finish_chunk(i, _):
        row0 = pl.multiple_of(i * CHUNK, 16)
        last_arrival(i, row0, CHUNK)
        multiply(row0, CHUNK)
        return 0

    lax.fori_loop(0, features // FEATURE_TILE, partial_tile, 0)
    lax.fori_loop(0, full, finish_chunk, 0)
    last_arrival(full, full * CHUNK, rest)
    lax.fori_loop(0, features // FEATURE_TILE, last_tile, 0)

    for c, (row0, size) in enumerate(chunks):
        for h in range(heads):
            own_inner(h, c, row0, size).wait_send()

    @pl.when(is_middle)
    def _():
        for k in range(2):
            raw_copy(k).wait_send()
        text_outer().wait_send()
        stat_outer().wait_send()
        for c, (row0, size) in enumerate(chunks):
            own_outer(c, row0, size).wait_send()
            for h in range(heads):
                inner_outer(h, c, row0, size).wait_send()
            outer_inner(c, row0, size).wait_send()
            far_outer(c, row0, size).wait_send()

    @pl.when(is_end)
    def _():
        for j, peer in enumerate(seq_peers):
            text_copy(extra, seq, peer, j).wait_send()

    for j, peer in enumerate(seq_peers):
        for h in range(heads):
            text_copy(h, seq, peer, j).wait_send()
            stat_copy(h, seq, peer, j).wait_send()
        weight_copy(seq, peer, j).wait_send()
        relay_copy(peer, j, img).wait_send()


def body_kernel(
    sizes,
    queries,
    out_grad,
    token_image,
    unnormed_keys,
    values,
    key_gain,
    tile_count,
    key_projection_matrix,
    value_projection_matrix,
):
    n_seq, n_dp, heads, group = sizes
    rows, width = unnormed_keys.shape[1:]
    features = key_projection_matrix.shape[0]
    query_rows = n_seq * group * CAP
    chunk_count = rows // CHUNK + 1
    padded = -(-rows // 16) * 16
    vmem = pl.BlockSpec(memory_space=pltpu.VMEM)
    anywhere = pl.BlockSpec(memory_space=pltpu.HBM)
    dma = pltpu.SemaphoreType.DMA
    result = pl.pallas_call(
        functools.partial(kernel, sizes),
        out_shape=pltpu.VMEM((rows, features), jnp.bfloat16),
        in_specs=[
            vmem,
            pl.BlockSpec(memory_space=pltpu.SMEM),
            anywhere,
            anywhere,
            anywhere,
            anywhere,
            vmem,
            anywhere,
            anywhere,
        ],
        out_specs=vmem,
        scratch_shapes=[
            pltpu.VMEM(queries.shape, jnp.bfloat16),
            pltpu.VMEM(queries.shape, jnp.bfloat16),
            pltpu.VMEM((rows, width), jnp.bfloat16),
            pltpu.VMEM((rows, width), jnp.bfloat16),
            pltpu.VMEM((rows, width), jnp.bfloat16),
            pltpu.VMEM((2, rows, HEAD_WIDTH), jnp.bfloat16),
            pltpu.VMEM((rows % CHUNK, features), jnp.float32),
            pltpu.VMEM((n_seq, heads + 1, 2, group * CAP, HEAD_WIDTH), jnp.bfloat16),
            pltpu.VMEM((heads, rows, query_rows), jnp.float32),
            pltpu.VMEM((heads, rows, query_rows), jnp.float32),
            pltpu.VMEM((n_seq, heads, 8, query_rows), jnp.float32),
            pltpu.VMEM((2, 8, query_rows), jnp.float32),
            pltpu.VMEM((n_dp, padded, 2 * width), jnp.bfloat16),
            pltpu.VMEM((n_seq, features, 2 * width), jnp.bfloat16),
            dma((4,)),
            dma((heads + 1, n_seq - 1)),
            dma((heads + 1, n_seq)),
            dma((heads, n_seq - 1)),
            dma((heads, n_seq)),
            dma((2, heads)),
            dma((n_seq - 1,)),
            dma((n_seq,)),
            dma((n_seq - 1,)),
            dma((n_seq,)),
            dma((7, chunk_count)),
            dma((n_dp, 2, chunk_count)),
            dma((4,)),
            dma((3,)),
        ],
        compiler_params=pltpu.CompilerParams(
            collective_id=0, has_side_effects=True, vmem_limit_bytes=VMEM_BYTES - 2 * rows * features
        ),
    )(
        token_image[None],
        tile_count,
        queries,
        out_grad,
        unnormed_keys[0],
        values[0],
        key_gain[None],
        key_projection_matrix,
        value_projection_matrix,
    )
    return result[None]


def body(*args):
    n_seq, n_img, n_dp = (lax.axis_size(name) for name in ("seq", "img", "dp"))
    rows, width = args[3].shape[1:]
    heads = width // HEAD_WIDTH
    group = args[0].shape[1] // width
    fits = n_img == heads == 2 and n_seq == n_dp == 4 and args[7].shape[1] == width and rows % 8 == 0
    if fits and rows % CHUNK and rows % CHUNK % 16 == 8:
        return body_kernel((n_seq, n_dp, heads, group), *args)
    return body_any(*args)


def solution(mesh):
    in_specs = (
        P("seq", "dp"),
        P("seq", "dp"),
        P("seq"),
        P("img", "seq", "dp"),
        P("img", "seq", "dp"),
        P(),
        P(),
        P("dp", "seq"),
        P("dp", "seq"),
    )
    out_specs = P("img", "seq", "dp")
    return jax.shard_map(body, mesh=mesh, in_specs=in_specs, out_specs=out_specs, check_vma=False)
```

```python
import functools

import jax
import jax.numpy as jnp
from jax import lax
from jax.experimental import pallas as pl
from jax.experimental.pallas import tpu as pltpu
from jax.sharding import PartitionSpec as P

QUERY_HEAD_COUNT = 64
KEY_VALUE_HEADS = 8
HEAD_WIDTH = 128
TILE_TOK = 1601
TILE_ROWS = 1608
CAP = 16


epsilon = 1e-05
masked = -1e30


def body_any(
    queries,
    out_grad,
    token_image,
    unnormed_keys,
    values,
    key_gain,
    tile_count,
    key_projection_matrix,
    value_projection_matrix,
):
    image_number = lax.axis_index("img")
    seq_index = lax.axis_index("seq")
    attends = token_image == image_number
    slot_rank = jnp.cumsum(attends.astype(jnp.int32)) - 1
    picker = (
        attends[None, :] & (slot_rank[None, :] == jnp.arange(CAP, dtype=jnp.int32)[:, None])
    ).astype(jnp.bfloat16)
    packed_query = jnp.dot(picker, queries, preferred_element_type=jnp.float32).astype(jnp.bfloat16)
    packed_grad = jnp.dot(picker, out_grad, preferred_element_type=jnp.float32).astype(jnp.bfloat16)
    text_query, text_grad = (
        lax.all_gather(packed_query, "seq", axis=0, tiled=True),
        lax.all_gather(packed_grad, "seq", axis=0, tiled=True),
    )
    key_rows = unnormed_keys.shape[1]
    key_width = unnormed_keys.shape[2]
    key_heads = key_width // HEAD_WIDTH
    group_length = QUERY_HEAD_COUNT // KEY_VALUE_HEADS
    text_rows = text_query.shape[0]
    score_scale = HEAD_WIDTH ** (-0.5)
    unnormed_float = unnormed_keys[0].astype(jnp.float32).reshape(key_rows, key_heads, HEAD_WIDTH)
    inverse = lax.rsqrt(jnp.mean(unnormed_float * unnormed_float, axis=-1, keepdims=True) + epsilon)
    unit_key = unnormed_float * inverse
    normed = (unit_key * key_gain).astype(jnp.bfloat16)
    value_heads = values[0].reshape(key_rows, key_heads, HEAD_WIDTH)
    query_heads = text_query.reshape(text_rows, key_heads, group_length, HEAD_WIDTH)
    grad_heads = text_grad.reshape(text_rows, key_heads, group_length, HEAD_WIDTH)
    row_global = seq_index * key_rows + jnp.arange(key_rows, dtype=jnp.int32)
    tile_limit = jnp.sum(
        jnp.where(jnp.arange(tile_count.shape[0], dtype=jnp.int32) == image_number, tile_count, 0)
    )
    live_rows = (row_global // TILE_ROWS < tile_limit) & (row_global % TILE_ROWS < TILE_TOK)
    scores = (
        jnp.einsum("rhge,khe->hgrk", query_heads, normed, preferred_element_type=jnp.float32)
        * score_scale
    )
    scores = jnp.where(live_rows, scores, masked)
    grad_probs = jnp.einsum(
        "rhge,khe->hgrk", grad_heads, value_heads, preferred_element_type=jnp.float32
    )
    row_top = lax.pmax(jnp.max(scores, axis=-1), "seq")
    exponent = jnp.exp(scores - row_top[..., None])
    row_total = lax.psum(jnp.sum(exponent, axis=-1), "seq")
    probabilities = exponent / row_total[..., None]
    inner_sum = lax.psum(jnp.sum(probabilities * grad_probs, axis=-1), "seq")
    probs_low = probabilities.astype(jnp.bfloat16)
    score_grad = (probabilities * (grad_probs - inner_sum[..., None])).astype(jnp.bfloat16)
    value_gradient = jnp.einsum(
        "hgrk,rhge->khe", probs_low, grad_heads, preferred_element_type=jnp.float32
    )
    normalized_gradient = (
        jnp.einsum("hgrk,rhge->khe", score_grad, query_heads, preferred_element_type=jnp.float32)
        * score_scale
    )
    unit_grad = normalized_gradient * key_gain
    key_gradient = inverse * (
        unit_grad - unit_key * jnp.mean(unit_grad * unit_key, axis=-1, keepdims=True)
    )
    key_reduced_precision = key_gradient.astype(jnp.bfloat16).reshape(key_rows, key_width)
    value_reduced_precision = value_gradient.astype(jnp.bfloat16).reshape(key_rows, key_width)
    key_all, value_all = (
        lax.all_gather(key_reduced_precision, "dp", axis=1, tiled=True),
        lax.all_gather(value_reduced_precision, "dp", axis=1, tiled=True),
    )
    contracting = (((1,), (1,)), ((), ()))
    partial_value = lax.dot_general(
        key_all,
        lax.all_gather(key_projection_matrix, "seq", axis=1, tiled=True),
        contracting,
        preferred_element_type=jnp.float32,
    )
    feature_sum = partial_value + lax.dot_general(
        value_all,
        lax.all_gather(value_projection_matrix, "seq", axis=1, tiled=True),
        contracting,
        preferred_element_type=jnp.float32,
    )
    return feature_sum.astype(jnp.bfloat16)[None]


MESH = pl.DeviceIdType.MESH
NT = (((1,), (1,)), ((), ()))
NN = (((1,), (0,)), ((), ()))
CHUNK = 272
FEATURE_TILE = 256
VMEM_BYTES = 67043328


def dot(a, b, dims):
    return lax.dot_general(a, b, dims, preferred_element_type=jnp.float32)


def kernel(
    sizes,
    image_ref,
    limit_ref,
    query_hbm,
    grad_hbm,
    key_hbm,
    value_hbm,
    gain_ref,
    key_weight_ref,
    value_weight_ref,
    out_ref,
    query_ref,
    grad_ref,
    key_ref,
    value_ref,
    normed_ref,
    raw,
    partial,
    text,
    score,
    grad_prob,
    stats,
    outer_stats,
    rows_all,
    weights,
    load_sem,
    text_send,
    text_recv,
    stat_send,
    stat_recv,
    weight_local,
    weight_send,
    weight_recv,
    relay_send,
    relay_recv,
    row_send,
    row_recv,
    raw_send,
    raw_recv,
):
    n_seq, n_dp, heads, group = sizes
    seq = lax.axis_index("seq")
    img = lax.axis_index("img")
    dp = lax.axis_index("dp")
    rows, width = key_ref.shape
    features = key_weight_ref.shape[0]
    half = features // 2
    stack = group * CAP
    query_rows = n_seq * stack
    full = rows // CHUNK
    rest = rows - full * CHUNK
    chunks = [(c * CHUNK, CHUNK) for c in range(full)] + [(full * CHUNK, rest)]
    scale = HEAD_WIDTH ** (-0.5)
    near, far = seq % 2, seq // 2
    seq_peers = [far * 2 + 1 - near, (1 - far) * 2 + near, (1 - far) * 2 + 1 - near]
    step = 1 - 2 * (dp // 2)
    inner, outer, second = dp + step, dp - step, dp + 2 * step
    farthest = (n_dp - 1) * (1 - dp // 2)
    is_end = (dp == 0) | (dp == n_dp - 1)
    is_middle = (dp > 0) & (dp < n_dp - 1)
    extra = heads

    loads = [
        pltpu.make_async_copy(source, target, load_sem.at[k])
        for k, (source, target) in enumerate(
            (
                (query_hbm, query_ref),
                (grad_hbm, grad_ref),
                (key_hbm, key_ref),
                (value_hbm, value_ref),
            )
        )
    ]
    for copy in loads:
        copy.start()

    barrier = pltpu.get_barrier_semaphore()
    for peer in seq_peers:
        pl.semaphore_signal(barrier, inc=1, device_id={"seq": peer}, device_id_type=MESH)
    pl.semaphore_signal(barrier, inc=1, device_id={"img": 1 - img}, device_id_type=MESH)
    pl.semaphore_signal(barrier, inc=1, device_id={"dp": inner}, device_id_type=MESH)

    @pl.when(is_middle)
    def _():
        pl.semaphore_signal(barrier, inc=1, device_id={"dp": outer}, device_id_type=MESH)

    def raw_copy(k):
        source = (key_hbm, value_hbm)[k]
        return pltpu.make_async_remote_copy(
            src_ref=source.at[:, pl.ds(HEAD_WIDTH, HEAD_WIDTH)],
            dst_ref=raw.at[k],
            send_sem=raw_send.at[k],
            recv_sem=raw_recv.at[k],
            device_id={"dp": outer},
            device_id_type=MESH,
        )

    pl.semaphore_wait(barrier, n_seq - 1 + 1 + 1 + is_middle.astype(jnp.int32))

    @pl.when(is_middle)
    def _():
        raw_copy(0).start()

    own_weights = [
        pltpu.make_async_copy(
            ref.at[:, pl.ds(h * HEAD_WIDTH, HEAD_WIDTH)],
            weights.at[seq, :, pl.ds((2 * h + k) * HEAD_WIDTH, HEAD_WIDTH)],
            weight_local.at[k, h],
        )
        for k, ref in enumerate((key_weight_ref, value_weight_ref))
        for h in range(heads)
    ]
    for copy in own_weights:
        copy.start()

    tokens = image_ref.shape[1]
    attends = image_ref[...] == img
    upper = (
        lax.broadcasted_iota(jnp.int32, (tokens, tokens), 0)
        <= lax.broadcasted_iota(jnp.int32, (tokens, tokens), 1)
    ).astype(jnp.bfloat16)
    counts = dot(
        jnp.broadcast_to(attends.astype(jnp.float32), (CAP, tokens)).astype(jnp.bfloat16), upper, NN
    )
    slot = lax.broadcasted_iota(jnp.int32, (CAP, tokens), 0).astype(jnp.float32) + 1.0
    picker = jnp.where(attends & (counts == slot), 1.0, 0.0).astype(jnp.bfloat16)

    def text_outer():
        return pltpu.make_async_remote_copy(
            src_ref=text.at[seq, heads - 1],
            dst_ref=text.at[seq, extra],
            send_sem=raw_send.at[2],
            recv_sem=text_recv.at[extra, seq],
            device_id={"dp": outer},
            device_id_type=MESH,
        )

    def stat_outer():
        return pltpu.make_async_remote_copy(
            src_ref=outer_stats.at[0],
            dst_ref=outer_stats.at[1],
            send_sem=raw_send.at[3],
            recv_sem=raw_recv.at[2],
            device_id={"dp": outer},
            device_id_type=MESH,
        )

    def text_copy(h, owner, peer, j):
        return pltpu.make_async_remote_copy(
            src_ref=text.at[owner, h],
            dst_ref=text.at[owner, h],
            send_sem=text_send.at[h, j],
            recv_sem=text_recv.at[h, owner],
            device_id={"seq": peer},
            device_id_type=MESH,
        )

    for copy in loads[:2]:
        copy.wait()
    for h in range(heads):
        for k, ref in enumerate((query_ref, grad_ref)):
            first = h * group * HEAD_WIDTH
            packed = dot(picker, ref[:, first : first + group * HEAD_WIDTH], NN).astype(jnp.bfloat16)
            for g in range(group):
                column = g * HEAD_WIDTH
                text[seq, h, k, g * CAP : (g + 1) * CAP, :] = packed[:, column : column + HEAD_WIDTH]
        for j, peer in enumerate(seq_peers):
            text_copy(h, seq, peer, j).start()

    @pl.when(is_middle)
    def _():
        text_outer().start()
        raw_copy(1).start()

    gain = gain_ref[...]
    live_limit = limit_ref[img]

    def unit_of(k):
        inverse = lax.rsqrt(jnp.mean(k * k, axis=-1, keepdims=True) + epsilon)
        return k * inverse, inverse

    def own_key(row0, size, h):
        return key_ref[pl.ds(row0, size), h * HEAD_WIDTH : (h + 1) * HEAD_WIDTH].astype(jnp.float32)

    def text_of(h, k):
        return text[:, h, k].reshape(query_rows, HEAD_WIDTH)

    def live_of(row0, size):
        row = seq * rows + row0 + lax.broadcasted_iota(jnp.int32, (size, 1), 0)
        return (row // TILE_ROWS < live_limit) & (row % TILE_ROWS < TILE_TOK)

    def over_chunks(act, carry):
        carry = lax.fori_loop(
            0, full, lambda i, c: act(pl.multiple_of(i * CHUNK, 16), CHUNK, c), carry
        )
        return act(full * CHUNK, rest, carry)

    for copy in loads[2:]:
        copy.wait()

    def normalize_chunk(row0, size, carry):
        for h in range(heads):
            unit, _ = unit_of(own_key(row0, size, h))
            normed_ref[pl.ds(row0, size), h * HEAD_WIDTH : (h + 1) * HEAD_WIDTH] = (
                unit * gain
            ).astype(jnp.bfloat16)
        return carry

    over_chunks(normalize_chunk, 0)

    def stat_copy(h, owner, peer, j):
        return pltpu.make_async_remote_copy(
            src_ref=stats.at[owner, h],
            dst_ref=stats.at[owner, h],
            send_sem=stat_send.at[h, j],
            recv_sem=stat_recv.at[h, owner],
            device_id={"seq": peer},
            device_id_type=MESH,
        )

    for h in range(heads):
        lanes = slice(h * HEAD_WIDTH, (h + 1) * HEAD_WIDTH)
        for j, owner in enumerate(seq_peers):
            text_copy(h, owner, owner, j).wait_recv()

        def first_pass(row0, size, top):
            s = dot(normed_ref[pl.ds(row0, size), lanes], text_of(h, 0), NT) * scale
            s = jnp.where(live_of(row0, size), s, masked)
            score[h, pl.ds(row0, size), :] = s
            return jnp.maximum(top, jnp.max(s, axis=0, keepdims=True))

        top = over_chunks(first_pass, jnp.full((1, query_rows), masked, jnp.float32))

        def second_pass(row0, size, sums):
            e = jnp.exp(score[h, pl.ds(row0, size), :] - top)
            p = dot(value_ref[pl.ds(row0, size), lanes], text_of(h, 1), NT)
            score[h, pl.ds(row0, size), :] = e
            grad_prob[h, pl.ds(row0, size), :] = p
            return (
                sums[0] + jnp.sum(e, axis=0, keepdims=True),
                sums[1] + jnp.sum(e * p, axis=0, keepdims=True),
            )

        sums = over_chunks(
            second_pass, tuple(jnp.zeros((1, query_rows), jnp.float32) for _ in range(2))
        )
        stats[seq, h, 0:1, :] = top
        stats[seq, h, 1:2, :] = sums[0]
        stats[seq, h, 2:3, :] = sums[1]
        stats[seq, h, 3:8, :] = jnp.zeros((5, query_rows), jnp.float32)
        for j, peer in enumerate(seq_peers):
            stat_copy(h, seq, peer, j).start()

    @pl.when(is_end)
    def _():
        text_outer().wait_recv()
        for j, peer in enumerate(seq_peers):
            text_copy(extra, seq, peer, j).start()

    def weight_copy(owner, peer, j):
        part = weights.at[owner, pl.ds(pl.multiple_of(img * half, half), half)]
        return pltpu.make_async_remote_copy(
            src_ref=part,
            dst_ref=part,
            send_sem=weight_send.at[j],
            recv_sem=weight_recv.at[owner],
            device_id={"seq": peer},
            device_id_type=MESH,
        )

    def relay_copy(owner, j, which):
        part = weights.at[owner, pl.ds(pl.multiple_of(which * half, half), half)]
        return pltpu.make_async_remote_copy(
            src_ref=part,
            dst_ref=part,
            send_sem=relay_send.at[j],
            recv_sem=relay_recv.at[owner],
            device_id={"img": 1 - img},
            device_id_type=MESH,
        )

    for copy in own_weights:
        copy.wait()
    for j, peer in enumerate(seq_peers):
        weight_copy(seq, peer, j).start()

    def combine(h):
        for j, peer in enumerate(seq_peers):
            stat_copy(h, peer, peer, j).wait_recv()
        tops = [stats[i, h, 0:1, :] for i in range(n_seq)]
        top = functools.reduce(jnp.maximum, tops)
        factors = [jnp.exp(t - top) for t in tops]
        total = sum(f * stats[i, h, 1:2, :] for i, f in enumerate(factors))
        inner_sum = sum(f * stats[i, h, 2:3, :] for i, f in enumerate(factors)) / total
        own = jnp.exp(stats[seq, h, 0:1, :] - top) / total
        return top, 1.0 / total, inner_sum, own

    def row_copy(kind, owner, h, c, row0, size, peer):
        lane0, lanes = (0, 2 * width) if h is None else (2 * h * HEAD_WIDTH, 2 * HEAD_WIDTH)
        part = rows_all.at[owner, pl.ds(row0, size), pl.ds(lane0, lanes)]
        return pltpu.make_async_remote_copy(
            src_ref=part,
            dst_ref=part,
            send_sem=row_send.at[kind, c],
            recv_sem=row_recv.at[owner, 0 if h == 0 else 1, c],
            device_id={"dp": peer},
            device_id_type=MESH,
        )

    def arrive(owner, h, c, row0, size):
        row_copy(0, owner, h, c, row0, size, inner).wait_recv()

    def own_inner(h, c, row0, size):
        return row_copy(h, dp, h, c, row0, size, inner)

    def own_outer(c, row0, size):
        return row_copy(2, dp, 0, c, row0, size, outer)

    def inner_outer(h, c, row0, size):
        return row_copy(3 + h, inner, h, c, row0, size, outer)

    def far_outer(c, row0, size):
        return row_copy(5, farthest, None, c, row0, size, outer)

    def outer_inner(c, row0, size):
        return row_copy(6, outer, None, c, row0, size, inner)

    def finish(owner, h, which, row0, size, p, g, unit, inverse):
        value_gradient = dot(p.astype(jnp.bfloat16), text_of(which, 1), NN)
        unit_grad = dot(g.astype(jnp.bfloat16), text_of(which, 0), NN) * scale * gain
        key_gradient = inverse * (
            unit_grad - unit * jnp.mean(unit_grad * unit, axis=-1, keepdims=True)
        )
        lane = 2 * h * HEAD_WIDTH
        rows_all[owner, pl.ds(row0, size), lane : lane + HEAD_WIDTH] = key_gradient.astype(
            jnp.bfloat16
        )
        lane = lane + HEAD_WIDTH
        rows_all[owner, pl.ds(row0, size), lane : lane + HEAD_WIDTH] = value_gradient.astype(
            jnp.bfloat16
        )

    for h in range(heads):
        top, inverse_total, inner_sum, own_factor = combine(h)
        if h == heads - 1:
            outer_stats[0, 0:1, :] = top
            outer_stats[0, 1:2, :] = inverse_total
            outer_stats[0, 2:3, :] = inner_sum
            outer_stats[0, 3:8, :] = jnp.zeros((5, query_rows), jnp.float32)

            @pl.when(is_middle)
            def _():
                stat_outer().start()

        def own_pass(c, row0, size):
            p = score[h, pl.ds(row0, size), :] * own_factor
            g = p * (grad_prob[h, pl.ds(row0, size), :] - inner_sum)
            finish(dp, h, h, row0, size, p, g, *unit_of(own_key(row0, size, h)))
            own_inner(h, c, row0, size).start()
            if h == 0:

                @pl.when(is_middle)
                def _():
                    own_outer(c, row0, size).start()

        def own_chunk(i, _):
            own_pass(i, pl.multiple_of(i * CHUNK, 16), CHUNK)
            return 0

        lax.fori_loop(0, full, own_chunk, 0)
        own_pass(full, full * CHUNK, rest)

    @pl.when(is_middle)
    def _():
        for c, (row0, size) in enumerate(chunks):
            arrive(outer, 0, c, row0, size)
            arrive(inner, 0, c, row0, size)
            inner_outer(0, c, row0, size).start()
        for c, (row0, size) in enumerate(chunks):
            arrive(inner, 1, c, row0, size)
            inner_outer(1, c, row0, size).start()
            arrive(outer, 1, c, row0, size)
            outer_inner(c, row0, size).start()

    @pl.when(is_end)
    def _():
        for j, owner in enumerate(seq_peers):
            text_copy(extra, owner, owner, j).wait_recv()
        for k in range(2):
            raw_copy(k).wait_recv()
        stat_outer().wait_recv()
        top = outer_stats[1, 0:1, :]
        inverse_total = outer_stats[1, 1:2, :]
        inner_sum = outer_stats[1, 2:3, :]

        def extra_pass(row0, size, carry):
            unit, inverse = unit_of(raw[0, pl.ds(row0, size), :].astype(jnp.float32))
            s = dot((unit * gain).astype(jnp.bfloat16), text_of(extra, 0), NT) * scale
            s = jnp.where(live_of(row0, size), s, masked)
            p = jnp.exp(s - top) * inverse_total
            g = p * (dot(raw[1, pl.ds(row0, size), :], text_of(extra, 1), NT) - inner_sum)
            finish(inner, heads - 1, extra, row0, size, p, g, unit, inverse)
            return carry

        over_chunks(extra_pass, 0)

    for j, peer in enumerate(seq_peers):
        weight_copy(peer, peer, j).wait_recv()
        relay_copy(peer, j, img).start()

    @pl.when(is_end)
    def _():
        for c, (row0, size) in enumerate(chunks):
            arrive(inner, 0, c, row0, size)
        for h in range(heads):
            for c, (row0, size) in enumerate(chunks):
                arrive(second, h, c, row0, size)

    for j, peer in enumerate(seq_peers):
        relay_copy(peer, j, 1 - img).wait_recv()

    def last_product(block, column):
        return dot(
            rows_all[block, full * CHUNK : rows, :],
            weights[block, pl.ds(column, FEATURE_TILE), :],
            NT,
        )

    def partial_tile(i, _):
        column = pl.multiple_of(i * FEATURE_TILE, FEATURE_TILE)
        partial[:, pl.ds(column, FEATURE_TILE)] = functools.reduce(
            jnp.add, [last_product(dp // 2 + b, column) for b in range(n_dp - 1)]
        )
        return 0

    def last_tile(i, _):
        column = pl.multiple_of(i * FEATURE_TILE, FEATURE_TILE)
        total = partial[:, pl.ds(column, FEATURE_TILE)] + last_product(farthest, column)
        out_ref[full * CHUNK : rows, pl.ds(column, FEATURE_TILE)] = total.astype(out_ref.dtype)
        return 0

    def multiply(row0, size):
        def tile(i, _):
            column = pl.multiple_of(i * FEATURE_TILE, FEATURE_TILE)
            total = functools.reduce(
                jnp.add,
                [
                    dot(
                        rows_all[b, pl.ds(row0, size), :],
                        weights[b, pl.ds(column, FEATURE_TILE), :],
                        NT,
                    )
                    for b in range(n_dp)
                ],
            )
            out_ref[pl.ds(row0, size), pl.ds(column, FEATURE_TILE)] = total.astype(out_ref.dtype)
            return 0

        lax.fori_loop(0, features // FEATURE_TILE, tile, 0)

    def last_arrival(c, row0, size):
        arrive(farthest, None, c, row0, size)

        @pl.when(is_middle)
        def _():
            far_outer(c, row0, size).start()

    def finish_chunk(i, _):
        row0 = pl.multiple_of(i * CHUNK, 16)
        last_arrival(i, row0, CHUNK)
        multiply(row0, CHUNK)
        return 0

    lax.fori_loop(0, features // FEATURE_TILE, partial_tile, 0)
    lax.fori_loop(0, full, finish_chunk, 0)
    last_arrival(full, full * CHUNK, rest)
    lax.fori_loop(0, features // FEATURE_TILE, last_tile, 0, unroll=True)

    for c, (row0, size) in enumerate(chunks):
        for h in range(heads):
            own_inner(h, c, row0, size).wait_send()

    @pl.when(is_middle)
    def _():
        for k in range(2):
            raw_copy(k).wait_send()
        text_outer().wait_send()
        stat_outer().wait_send()
        for c, (row0, size) in enumerate(chunks):
            own_outer(c, row0, size).wait_send()
            for h in range(heads):
                inner_outer(h, c, row0, size).wait_send()
            outer_inner(c, row0, size).wait_send()
            far_outer(c, row0, size).wait_send()

    @pl.when(is_end)
    def _():
        for j, peer in enumerate(seq_peers):
            text_copy(extra, seq, peer, j).wait_send()

    for j, peer in enumerate(seq_peers):
        for h in range(heads):
            text_copy(h, seq, peer, j).wait_send()
            stat_copy(h, seq, peer, j).wait_send()
        weight_copy(seq, peer, j).wait_send()
        relay_copy(peer, j, img).wait_send()


def body_kernel(
    sizes,
    queries,
    out_grad,
    token_image,
    unnormed_keys,
    values,
    key_gain,
    tile_count,
    key_projection_matrix,
    value_projection_matrix,
):
    n_seq, n_dp, heads, group = sizes
    rows, width = unnormed_keys.shape[1:]
    features = key_projection_matrix.shape[0]
    query_rows = n_seq * group * CAP
    chunk_count = rows // CHUNK + 1
    padded = -(-rows // 16) * 16
    vmem = pl.BlockSpec(memory_space=pltpu.VMEM)
    anywhere = pl.BlockSpec(memory_space=pltpu.HBM)
    dma = pltpu.SemaphoreType.DMA
    result = pl.pallas_call(
        functools.partial(kernel, sizes),
        out_shape=pltpu.VMEM((rows, features), jnp.bfloat16),
        in_specs=[
            vmem,
            pl.BlockSpec(memory_space=pltpu.SMEM),
            anywhere,
            anywhere,
            anywhere,
            anywhere,
            vmem,
            anywhere,
            anywhere,
        ],
        out_specs=vmem,
        scratch_shapes=[
            pltpu.VMEM(queries.shape, jnp.bfloat16),
            pltpu.VMEM(queries.shape, jnp.bfloat16),
            pltpu.VMEM((rows, width), jnp.bfloat16),
            pltpu.VMEM((rows, width), jnp.bfloat16),
            pltpu.VMEM((rows, width), jnp.bfloat16),
            pltpu.VMEM((2, rows, HEAD_WIDTH), jnp.bfloat16),
            pltpu.VMEM((rows % CHUNK, features), jnp.float32),
            pltpu.VMEM((n_seq, heads + 1, 2, group * CAP, HEAD_WIDTH), jnp.bfloat16),
            pltpu.VMEM((heads, rows, query_rows), jnp.float32),
            pltpu.VMEM((heads, rows, query_rows), jnp.float32),
            pltpu.VMEM((n_seq, heads, 8, query_rows), jnp.float32),
            pltpu.VMEM((2, 8, query_rows), jnp.float32),
            pltpu.VMEM((n_dp, padded, 2 * width), jnp.bfloat16),
            pltpu.VMEM((n_seq, features, 2 * width), jnp.bfloat16),
            dma((4,)),
            dma((heads + 1, n_seq - 1)),
            dma((heads + 1, n_seq)),
            dma((heads, n_seq - 1)),
            dma((heads, n_seq)),
            dma((2, heads)),
            dma((n_seq - 1,)),
            dma((n_seq,)),
            dma((n_seq - 1,)),
            dma((n_seq,)),
            dma((7, chunk_count)),
            dma((n_dp, 2, chunk_count)),
            dma((4,)),
            dma((3,)),
        ],
        compiler_params=pltpu.CompilerParams(
            collective_id=0, has_side_effects=True, vmem_limit_bytes=VMEM_BYTES - 2 * rows * features
        ),
    )(
        token_image[None],
        tile_count,
        queries,
        out_grad,
        unnormed_keys[0],
        values[0],
        key_gain[None],
        key_projection_matrix,
        value_projection_matrix,
    )
    return result[None]


def body(*args):
    n_seq, n_img, n_dp = (lax.axis_size(name) for name in ("seq", "img", "dp"))
    rows, width = args[3].shape[1:]
    heads = width // HEAD_WIDTH
    group = args[0].shape[1] // width
    fits = n_img == heads == 2 and n_seq == n_dp == 4 and args[7].shape[1] == width and rows % 8 == 0
    if fits and rows % CHUNK and rows % CHUNK % 16 == 8:
        return body_kernel((n_seq, n_dp, heads, group), *args)
    return body_any(*args)


def solution(mesh):
    in_specs = (
        P("seq", "dp"),
        P("seq", "dp"),
        P("seq"),
        P("img", "seq", "dp"),
        P("img", "seq", "dp"),
        P(),
        P(),
        P("dp", "seq"),
        P("dp", "seq"),
    )
    out_specs = P("img", "seq", "dp")
    return jax.shard_map(body, mesh=mesh, in_specs=in_specs, out_specs=out_specs, check_vma=False)
```

```python
import functools

import jax
import jax.numpy as jnp
from jax import lax
from jax.experimental import pallas as pl
from jax.experimental.pallas import tpu as pltpu
from jax.sharding import PartitionSpec as P

QUERY_HEAD_COUNT = 64
KEY_VALUE_HEADS = 8
HEAD_WIDTH = 128
TILE_TOK = 1601
TILE_ROWS = 1608
CAP = 16


epsilon = 1e-05
masked = -1e30


def body_any(
    queries,
    out_grad,
    token_image,
    unnormed_keys,
    values,
    key_gain,
    tile_count,
    key_projection_matrix,
    value_projection_matrix,
):
    image_number = lax.axis_index("img")
    seq_index = lax.axis_index("seq")
    attends = token_image == image_number
    slot_rank = jnp.cumsum(attends.astype(jnp.int32)) - 1
    picker = (
        attends[None, :] & (slot_rank[None, :] == jnp.arange(CAP, dtype=jnp.int32)[:, None])
    ).astype(jnp.bfloat16)
    packed_query = jnp.dot(picker, queries, preferred_element_type=jnp.float32).astype(jnp.bfloat16)
    packed_grad = jnp.dot(picker, out_grad, preferred_element_type=jnp.float32).astype(jnp.bfloat16)
    text_query, text_grad = (
        lax.all_gather(packed_query, "seq", axis=0, tiled=True),
        lax.all_gather(packed_grad, "seq", axis=0, tiled=True),
    )
    key_rows = unnormed_keys.shape[1]
    key_width = unnormed_keys.shape[2]
    key_heads = key_width // HEAD_WIDTH
    group_length = QUERY_HEAD_COUNT // KEY_VALUE_HEADS
    text_rows = text_query.shape[0]
    score_scale = HEAD_WIDTH ** (-0.5)
    unnormed_float = unnormed_keys[0].astype(jnp.float32).reshape(key_rows, key_heads, HEAD_WIDTH)
    inverse = lax.rsqrt(jnp.mean(unnormed_float * unnormed_float, axis=-1, keepdims=True) + epsilon)
    unit_key = unnormed_float * inverse
    normed = (unit_key * key_gain).astype(jnp.bfloat16)
    value_heads = values[0].reshape(key_rows, key_heads, HEAD_WIDTH)
    query_heads = text_query.reshape(text_rows, key_heads, group_length, HEAD_WIDTH)
    grad_heads = text_grad.reshape(text_rows, key_heads, group_length, HEAD_WIDTH)
    row_global = seq_index * key_rows + jnp.arange(key_rows, dtype=jnp.int32)
    tile_limit = jnp.sum(
        jnp.where(jnp.arange(tile_count.shape[0], dtype=jnp.int32) == image_number, tile_count, 0)
    )
    live_rows = (row_global // TILE_ROWS < tile_limit) & (row_global % TILE_ROWS < TILE_TOK)
    scores = (
        jnp.einsum("rhge,khe->hgrk", query_heads, normed, preferred_element_type=jnp.float32)
        * score_scale
    )
    scores = jnp.where(live_rows, scores, masked)
    grad_probs = jnp.einsum(
        "rhge,khe->hgrk", grad_heads, value_heads, preferred_element_type=jnp.float32
    )
    row_top = lax.pmax(jnp.max(scores, axis=-1), "seq")
    exponent = jnp.exp(scores - row_top[..., None])
    row_total = lax.psum(jnp.sum(exponent, axis=-1), "seq")
    probabilities = exponent / row_total[..., None]
    inner_sum = lax.psum(jnp.sum(probabilities * grad_probs, axis=-1), "seq")
    probs_low = probabilities.astype(jnp.bfloat16)
    score_grad = (probabilities * (grad_probs - inner_sum[..., None])).astype(jnp.bfloat16)
    value_gradient = jnp.einsum(
        "hgrk,rhge->khe", probs_low, grad_heads, preferred_element_type=jnp.float32
    )
    normalized_gradient = (
        jnp.einsum("hgrk,rhge->khe", score_grad, query_heads, preferred_element_type=jnp.float32)
        * score_scale
    )
    unit_grad = normalized_gradient * key_gain
    key_gradient = inverse * (
        unit_grad - unit_key * jnp.mean(unit_grad * unit_key, axis=-1, keepdims=True)
    )
    key_reduced_precision = key_gradient.astype(jnp.bfloat16).reshape(key_rows, key_width)
    value_reduced_precision = value_gradient.astype(jnp.bfloat16).reshape(key_rows, key_width)
    key_all, value_all = (
        lax.all_gather(key_reduced_precision, "dp", axis=1, tiled=True),
        lax.all_gather(value_reduced_precision, "dp", axis=1, tiled=True),
    )
    contracting = (((1,), (1,)), ((), ()))
    partial_value = lax.dot_general(
        key_all,
        lax.all_gather(key_projection_matrix, "seq", axis=1, tiled=True),
        contracting,
        preferred_element_type=jnp.float32,
    )
    feature_sum = partial_value + lax.dot_general(
        value_all,
        lax.all_gather(value_projection_matrix, "seq", axis=1, tiled=True),
        contracting,
        preferred_element_type=jnp.float32,
    )
    return feature_sum.astype(jnp.bfloat16)[None]


MESH = pl.DeviceIdType.MESH
NT = (((1,), (1,)), ((), ()))
NN = (((1,), (0,)), ((), ()))
CHUNK = 272
FEATURE_TILE = 256
VMEM_BYTES = 67043328


def dot(a, b, dims):
    return lax.dot_general(a, b, dims, preferred_element_type=jnp.float32)


def kernel(
    sizes,
    image_ref,
    limit_ref,
    query_hbm,
    grad_hbm,
    key_hbm,
    value_hbm,
    gain_ref,
    key_weight_ref,
    value_weight_ref,
    out_ref,
    query_ref,
    grad_ref,
    key_ref,
    value_ref,
    normed_ref,
    raw,
    partial,
    text,
    score,
    grad_prob,
    stats,
    outer_stats,
    rows_all,
    weights,
    load_sem,
    text_send,
    text_recv,
    stat_send,
    stat_recv,
    weight_local,
    weight_send,
    weight_recv,
    relay_send,
    relay_recv,
    row_send,
    row_recv,
    raw_send,
    raw_recv,
    entered,
):
    n_seq, n_dp, heads, group = sizes
    seq = lax.axis_index("seq")
    img = lax.axis_index("img")
    dp = lax.axis_index("dp")
    rows, width = key_ref.shape
    features = key_weight_ref.shape[0]
    half = features // 2
    stack = group * CAP
    query_rows = n_seq * stack
    full = rows // CHUNK
    rest = rows - full * CHUNK
    chunks = [(c * CHUNK, CHUNK) for c in range(full)] + [(full * CHUNK, rest)]
    scale = HEAD_WIDTH ** (-0.5)
    near, far = seq % 2, seq // 2
    seq_peers = [far * 2 + 1 - near, (1 - far) * 2 + near, (1 - far) * 2 + 1 - near]
    step = 1 - 2 * (dp // 2)
    inner, outer, second = dp + step, dp - step, dp + 2 * step
    farthest = (n_dp - 1) * (1 - dp // 2)
    is_end = (dp == 0) | (dp == n_dp - 1)
    is_middle = (dp > 0) & (dp < n_dp - 1)
    extra = heads

    loads = [
        pltpu.make_async_copy(source, target, load_sem.at[k])
        for k, (source, target) in enumerate(
            (
                (query_hbm, query_ref),
                (grad_hbm, grad_ref),
                (key_hbm, key_ref),
                (value_hbm, value_ref),
            )
        )
    ]
    for copy in loads:
        copy.start()

    barrier = pltpu.get_barrier_semaphore()
    for peer in seq_peers[:2]:
        pl.semaphore_signal(barrier, inc=1, device_id={"seq": peer}, device_id_type=MESH)
    pl.semaphore_signal(barrier, inc=1, device_id={"img": 1 - img}, device_id_type=MESH)
    pl.semaphore_signal(barrier, inc=1, device_id={"dp": inner}, device_id_type=MESH)

    @pl.when(is_middle)
    def _():
        pl.semaphore_signal(barrier, inc=1, device_id={"dp": outer}, device_id_type=MESH)

    def raw_copy(k):
        source = (key_hbm, value_hbm)[k]
        return pltpu.make_async_remote_copy(
            src_ref=source.at[:, pl.ds(HEAD_WIDTH, HEAD_WIDTH)],
            dst_ref=raw.at[k],
            send_sem=raw_send.at[k],
            recv_sem=raw_recv.at[k],
            device_id={"dp": outer},
            device_id_type=MESH,
        )

    pl.semaphore_wait(barrier, 2 + 1 + 1 + is_middle.astype(jnp.int32))

    @pl.when(is_middle)
    def _():
        raw_copy(0).start()

    pl.semaphore_signal(entered, inc=1, device_id={"seq": seq_peers[0]}, device_id_type=MESH)

    own_weights = [
        pltpu.make_async_copy(
            ref.at[:, pl.ds(h * HEAD_WIDTH, HEAD_WIDTH)],
            weights.at[seq, :, pl.ds((2 * h + k) * HEAD_WIDTH, HEAD_WIDTH)],
            weight_local.at[k, h],
        )
        for k, ref in enumerate((key_weight_ref, value_weight_ref))
        for h in range(heads)
    ]
    for copy in own_weights:
        copy.start()

    tokens = image_ref.shape[1]
    attends = image_ref[...] == img
    upper = (
        lax.broadcasted_iota(jnp.int32, (tokens, tokens), 0)
        <= lax.broadcasted_iota(jnp.int32, (tokens, tokens), 1)
    ).astype(jnp.bfloat16)
    counts = dot(
        jnp.broadcast_to(attends.astype(jnp.float32), (CAP, tokens)).astype(jnp.bfloat16), upper, NN
    )
    slot = lax.broadcasted_iota(jnp.int32, (CAP, tokens), 0).astype(jnp.float32) + 1.0
    picker = jnp.where(attends & (counts == slot), 1.0, 0.0).astype(jnp.bfloat16)

    def text_outer():
        return pltpu.make_async_remote_copy(
            src_ref=text.at[seq, heads - 1],
            dst_ref=text.at[seq, extra],
            send_sem=raw_send.at[2],
            recv_sem=text_recv.at[extra, seq],
            device_id={"dp": outer},
            device_id_type=MESH,
        )

    def stat_outer():
        return pltpu.make_async_remote_copy(
            src_ref=outer_stats.at[0],
            dst_ref=outer_stats.at[1],
            send_sem=raw_send.at[3],
            recv_sem=raw_recv.at[2],
            device_id={"dp": outer},
            device_id_type=MESH,
        )

    def text_copy(h, owner, peer, j):
        return pltpu.make_async_remote_copy(
            src_ref=text.at[owner, h],
            dst_ref=text.at[owner, h],
            send_sem=text_send.at[h, j],
            recv_sem=text_recv.at[h, owner],
            device_id={"seq": peer},
            device_id_type=MESH,
        )

    for copy in loads[:2]:
        copy.wait()
    for h in range(heads):
        for k, ref in enumerate((query_ref, grad_ref)):
            first = h * group * HEAD_WIDTH
            packed = dot(picker, ref[:, first : first + group * HEAD_WIDTH], NN).astype(jnp.bfloat16)
            for g in range(group):
                column = g * HEAD_WIDTH
                text[seq, h, k, g * CAP : (g + 1) * CAP, :] = packed[:, column : column + HEAD_WIDTH]
        for j, peer in enumerate(seq_peers):
            if h == 0 and j == 2:
                pl.semaphore_wait(entered, 1)
            text_copy(h, seq, peer, j).start()

    @pl.when(is_middle)
    def _():
        text_outer().start()
        raw_copy(1).start()

    gain = gain_ref[...]
    live_limit = limit_ref[img]

    def unit_of(k):
        inverse = lax.rsqrt(jnp.mean(k * k, axis=-1, keepdims=True) + epsilon)
        return k * inverse, inverse

    def own_key(row0, size, h):
        return key_ref[pl.ds(row0, size), h * HEAD_WIDTH : (h + 1) * HEAD_WIDTH].astype(jnp.float32)

    def text_of(h, k):
        return text[:, h, k].reshape(query_rows, HEAD_WIDTH)

    def live_of(row0, size):
        row = seq * rows + row0 + lax.broadcasted_iota(jnp.int32, (size, 1), 0)
        return (row // TILE_ROWS < live_limit) & (row % TILE_ROWS < TILE_TOK)

    def over_chunks(act, carry):
        carry = lax.fori_loop(
            0, full, lambda i, c: act(pl.multiple_of(i * CHUNK, 16), CHUNK, c), carry
        )
        return act(full * CHUNK, rest, carry)

    for copy in loads[2:]:
        copy.wait()

    def normalize_chunk(row0, size, carry):
        for h in range(heads):
            unit, _ = unit_of(own_key(row0, size, h))
            normed_ref[pl.ds(row0, size), h * HEAD_WIDTH : (h + 1) * HEAD_WIDTH] = (
                unit * gain
            ).astype(jnp.bfloat16)
        return carry

    over_chunks(normalize_chunk, 0)

    def stat_copy(h, owner, peer, j):
        return pltpu.make_async_remote_copy(
            src_ref=stats.at[owner, h],
            dst_ref=stats.at[owner, h],
            send_sem=stat_send.at[h, j],
            recv_sem=stat_recv.at[h, owner],
            device_id={"seq": peer},
            device_id_type=MESH,
        )

    for h in range(heads):
        lanes = slice(h * HEAD_WIDTH, (h + 1) * HEAD_WIDTH)
        for j, owner in enumerate(seq_peers):
            text_copy(h, owner, owner, j).wait_recv()

        def first_pass(row0, size, top):
            s = dot(normed_ref[pl.ds(row0, size), lanes], text_of(h, 0), NT) * scale
            s = jnp.where(live_of(row0, size), s, masked)
            score[h, pl.ds(row0, size), :] = s
            return jnp.maximum(top, jnp.max(s, axis=0, keepdims=True))

        top = over_chunks(first_pass, jnp.full((1, query_rows), masked, jnp.float32))

        def second_pass(row0, size, sums):
            e = jnp.exp(score[h, pl.ds(row0, size), :] - top)
            p = dot(value_ref[pl.ds(row0, size), lanes], text_of(h, 1), NT)
            score[h, pl.ds(row0, size), :] = e
            grad_prob[h, pl.ds(row0, size), :] = p
            return (
                sums[0] + jnp.sum(e, axis=0, keepdims=True),
                sums[1] + jnp.sum(e * p, axis=0, keepdims=True),
            )

        sums = over_chunks(
            second_pass, tuple(jnp.zeros((1, query_rows), jnp.float32) for _ in range(2))
        )
        stats[seq, h, 0:1, :] = top
        stats[seq, h, 1:2, :] = sums[0]
        stats[seq, h, 2:3, :] = sums[1]
        stats[seq, h, 3:8, :] = jnp.zeros((5, query_rows), jnp.float32)
        for j, peer in enumerate(seq_peers):
            stat_copy(h, seq, peer, j).start()

    @pl.when(is_end)
    def _():
        text_outer().wait_recv()
        for j, peer in enumerate(seq_peers):
            text_copy(extra, seq, peer, j).start()

    def weight_copy(owner, peer, j):
        part = weights.at[owner, pl.ds(pl.multiple_of(img * half, half), half)]
        return pltpu.make_async_remote_copy(
            src_ref=part,
            dst_ref=part,
            send_sem=weight_send.at[j],
            recv_sem=weight_recv.at[owner],
            device_id={"seq": peer},
            device_id_type=MESH,
        )

    def relay_copy(owner, j, which):
        part = weights.at[owner, pl.ds(pl.multiple_of(which * half, half), half)]
        return pltpu.make_async_remote_copy(
            src_ref=part,
            dst_ref=part,
            send_sem=relay_send.at[j],
            recv_sem=relay_recv.at[owner],
            device_id={"img": 1 - img},
            device_id_type=MESH,
        )

    for copy in own_weights:
        copy.wait()
    for j, peer in enumerate(seq_peers):
        weight_copy(seq, peer, j).start()

    def combine(h):
        for j, peer in enumerate(seq_peers):
            stat_copy(h, peer, peer, j).wait_recv()
        tops = [stats[i, h, 0:1, :] for i in range(n_seq)]
        top = functools.reduce(jnp.maximum, tops)
        factors = [jnp.exp(t - top) for t in tops]
        total = sum(f * stats[i, h, 1:2, :] for i, f in enumerate(factors))
        inner_sum = sum(f * stats[i, h, 2:3, :] for i, f in enumerate(factors)) / total
        own = jnp.exp(stats[seq, h, 0:1, :] - top) / total
        return top + jnp.log(total), inner_sum, own

    def row_copy(kind, owner, h, c, row0, size, peer):
        lane0, lanes = (0, 2 * width) if h is None else (2 * h * HEAD_WIDTH, 2 * HEAD_WIDTH)
        part = rows_all.at[owner, pl.ds(row0, size), pl.ds(lane0, lanes)]
        return pltpu.make_async_remote_copy(
            src_ref=part,
            dst_ref=part,
            send_sem=row_send.at[kind, c],
            recv_sem=row_recv.at[owner, 0 if h == 0 else 1, c],
            device_id={"dp": peer},
            device_id_type=MESH,
        )

    def arrive(owner, h, c, row0, size):
        row_copy(0, owner, h, c, row0, size, inner).wait_recv()

    def own_inner(h, c, row0, size):
        return row_copy(h, dp, h, c, row0, size, inner)

    def own_outer(c, row0, size):
        return row_copy(2, dp, 0, c, row0, size, outer)

    def inner_outer(h, c, row0, size):
        return row_copy(3 + h, inner, h, c, row0, size, outer)

    def far_outer(c, row0, size):
        return row_copy(5, farthest, None, c, row0, size, outer)

    def outer_inner(c, row0, size):
        return row_copy(6, outer, None, c, row0, size, inner)

    def finish(owner, h, which, row0, size, p, g, unit, inverse):
        value_gradient = dot(p.astype(jnp.bfloat16), text_of(which, 1), NN)
        unit_grad = dot(g.astype(jnp.bfloat16), text_of(which, 0), NN) * scale * gain
        key_gradient = inverse * (
            unit_grad - unit * jnp.mean(unit_grad * unit, axis=-1, keepdims=True)
        )
        lane = 2 * h * HEAD_WIDTH
        rows_all[owner, pl.ds(row0, size), lane : lane + HEAD_WIDTH] = key_gradient.astype(
            jnp.bfloat16
        )
        lane = lane + HEAD_WIDTH
        rows_all[owner, pl.ds(row0, size), lane : lane + HEAD_WIDTH] = value_gradient.astype(
            jnp.bfloat16
        )

    for h in range(heads):
        log_total, inner_sum, own_factor = combine(h)
        if h == heads - 1:
            for i in range(n_seq):
                part = slice(i * stack, (i + 1) * stack)
                outer_stats[0, i : i + 1, :] = log_total[:, part]
                outer_stats[0, n_seq + i : n_seq + i + 1, :] = inner_sum[:, part]

            @pl.when(is_middle)
            def _():
                stat_outer().start()

        def own_pass(c, row0, size):
            p = score[h, pl.ds(row0, size), :] * own_factor
            g = p * (grad_prob[h, pl.ds(row0, size), :] - inner_sum)
            finish(dp, h, h, row0, size, p, g, *unit_of(own_key(row0, size, h)))
            own_inner(h, c, row0, size).start()
            if h == 0:

                @pl.when(is_middle)
                def _():
                    own_outer(c, row0, size).start()

        def own_chunk(i, _):
            own_pass(i, pl.multiple_of(i * CHUNK, 16), CHUNK)
            return 0

        lax.fori_loop(0, full, own_chunk, 0)
        own_pass(full, full * CHUNK, rest)

    @pl.when(is_middle)
    def _():
        for c, (row0, size) in enumerate(chunks):
            arrive(outer, 0, c, row0, size)
            arrive(inner, 0, c, row0, size)
            inner_outer(0, c, row0, size).start()
        for c, (row0, size) in enumerate(chunks):
            arrive(inner, 1, c, row0, size)
            inner_outer(1, c, row0, size).start()
            arrive(outer, 1, c, row0, size)
            outer_inner(c, row0, size).start()

    @pl.when(is_end)
    def _():
        for j, owner in enumerate(seq_peers):
            text_copy(extra, owner, owner, j).wait_recv()
        for k in range(2):
            raw_copy(k).wait_recv()
        stat_outer().wait_recv()
        log_total, inner_sum = (
            jnp.concatenate([outer_stats[1, i + j : i + j + 1, :] for j in range(n_seq)], axis=1)
            for i in (0, n_seq)
        )

        def extra_pass(row0, size, carry):
            unit, inverse = unit_of(raw[0, pl.ds(row0, size), :].astype(jnp.float32))
            s = dot((unit * gain).astype(jnp.bfloat16), text_of(extra, 0), NT) * scale
            s = jnp.where(live_of(row0, size), s, masked)
            p = jnp.exp(s - log_total)
            g = p * (dot(raw[1, pl.ds(row0, size), :], text_of(extra, 1), NT) - inner_sum)
            finish(inner, heads - 1, extra, row0, size, p, g, unit, inverse)
            return carry

        over_chunks(extra_pass, 0)

    for j, peer in enumerate(seq_peers):
        weight_copy(peer, peer, j).wait_recv()
        relay_copy(peer, j, img).start()

    @pl.when(is_end)
    def _():
        for c, (row0, size) in enumerate(chunks):
            arrive(inner, 0, c, row0, size)
        for h in range(heads):
            for c, (row0, size) in enumerate(chunks):
                arrive(second, h, c, row0, size)

    for j, peer in enumerate(seq_peers):
        relay_copy(peer, j, 1 - img).wait_recv()

    def last_product(block, column):
        return dot(
            rows_all[block, full * CHUNK : rows, :],
            weights[block, pl.ds(column, FEATURE_TILE), :],
            NT,
        )

    def partial_tile(i, _):
        column = pl.multiple_of(i * FEATURE_TILE, FEATURE_TILE)
        partial[:, pl.ds(column, FEATURE_TILE)] = functools.reduce(
            jnp.add, [last_product(dp // 2 + b, column) for b in range(n_dp - 1)]
        )
        return 0

    def last_tile(i, _):
        column = pl.multiple_of(i * FEATURE_TILE, FEATURE_TILE)
        total = partial[:, pl.ds(column, FEATURE_TILE)] + last_product(farthest, column)
        out_ref[full * CHUNK : rows, pl.ds(column, FEATURE_TILE)] = total.astype(out_ref.dtype)
        return 0

    def multiply(row0, size):
        def tile(i, _):
            column = pl.multiple_of(i * FEATURE_TILE, FEATURE_TILE)
            total = functools.reduce(
                jnp.add,
                [
                    dot(
                        rows_all[b, pl.ds(row0, size), :],
                        weights[b, pl.ds(column, FEATURE_TILE), :],
                        NT,
                    )
                    for b in range(n_dp)
                ],
            )
            out_ref[pl.ds(row0, size), pl.ds(column, FEATURE_TILE)] = total.astype(out_ref.dtype)
            return 0

        lax.fori_loop(0, features // FEATURE_TILE, tile, 0)

    def last_arrival(c, row0, size):
        arrive(farthest, None, c, row0, size)

        @pl.when(is_middle)
        def _():
            far_outer(c, row0, size).start()

    def finish_chunk(i, _):
        row0 = pl.multiple_of(i * CHUNK, 16)
        last_arrival(i, row0, CHUNK)
        multiply(row0, CHUNK)
        return 0

    lax.fori_loop(0, features // FEATURE_TILE, partial_tile, 0)
    lax.fori_loop(0, full, finish_chunk, 0)
    last_arrival(full, full * CHUNK, rest)
    lax.fori_loop(0, features // FEATURE_TILE, last_tile, 0, unroll=True)

    for c, (row0, size) in enumerate(chunks):
        for h in range(heads):
            own_inner(h, c, row0, size).wait_send()

    @pl.when(is_middle)
    def _():
        for k in range(2):
            raw_copy(k).wait_send()
        text_outer().wait_send()
        stat_outer().wait_send()
        for c, (row0, size) in enumerate(chunks):
            own_outer(c, row0, size).wait_send()
            for h in range(heads):
                inner_outer(h, c, row0, size).wait_send()
            outer_inner(c, row0, size).wait_send()
            far_outer(c, row0, size).wait_send()

    @pl.when(is_end)
    def _():
        for j, peer in enumerate(seq_peers):
            text_copy(extra, seq, peer, j).wait_send()

    for j, peer in enumerate(seq_peers):
        for h in range(heads):
            text_copy(h, seq, peer, j).wait_send()
            stat_copy(h, seq, peer, j).wait_send()
        weight_copy(seq, peer, j).wait_send()
        relay_copy(peer, j, img).wait_send()


def body_kernel(
    sizes,
    queries,
    out_grad,
    token_image,
    unnormed_keys,
    values,
    key_gain,
    tile_count,
    key_projection_matrix,
    value_projection_matrix,
):
    n_seq, n_dp, heads, group = sizes
    rows, width = unnormed_keys.shape[1:]
    features = key_projection_matrix.shape[0]
    query_rows = n_seq * group * CAP
    chunk_count = rows // CHUNK + 1
    padded = -(-rows // 16) * 16
    vmem = pl.BlockSpec(memory_space=pltpu.VMEM)
    anywhere = pl.BlockSpec(memory_space=pltpu.HBM)
    dma = pltpu.SemaphoreType.DMA
    result = pl.pallas_call(
        functools.partial(kernel, sizes),
        out_shape=pltpu.VMEM((rows, features), jnp.bfloat16),
        in_specs=[
            vmem,
            pl.BlockSpec(memory_space=pltpu.SMEM),
            anywhere,
            anywhere,
            anywhere,
            anywhere,
            vmem,
            anywhere,
            anywhere,
        ],
        out_specs=vmem,
        scratch_shapes=[
            pltpu.VMEM(queries.shape, jnp.bfloat16),
            pltpu.VMEM(queries.shape, jnp.bfloat16),
            pltpu.VMEM((rows, width), jnp.bfloat16),
            pltpu.VMEM((rows, width), jnp.bfloat16),
            pltpu.VMEM((rows, width), jnp.bfloat16),
            pltpu.VMEM((2, rows, HEAD_WIDTH), jnp.bfloat16),
            pltpu.VMEM((rows % CHUNK, features), jnp.float32),
            pltpu.VMEM((n_seq, heads + 1, 2, group * CAP, HEAD_WIDTH), jnp.bfloat16),
            pltpu.VMEM((heads, rows, query_rows), jnp.float32),
            pltpu.VMEM((heads, rows, query_rows), jnp.float32),
            pltpu.VMEM((n_seq, heads, 8, query_rows), jnp.float32),
            pltpu.VMEM((2, 2 * n_seq, group * CAP), jnp.float32),
            pltpu.VMEM((n_dp, padded, 2 * width), jnp.bfloat16),
            pltpu.VMEM((n_seq, features, 2 * width), jnp.bfloat16),
            dma((4,)),
            dma((heads + 1, n_seq - 1)),
            dma((heads + 1, n_seq)),
            dma((heads, n_seq - 1)),
            dma((heads, n_seq)),
            dma((2, heads)),
            dma((n_seq - 1,)),
            dma((n_seq,)),
            dma((n_seq - 1,)),
            dma((n_seq,)),
            dma((7, chunk_count)),
            dma((n_dp, 2, chunk_count)),
            dma((4,)),
            dma((3,)),
            pltpu.SemaphoreType.REGULAR,
        ],
        compiler_params=pltpu.CompilerParams(
            collective_id=0, has_side_effects=True, vmem_limit_bytes=VMEM_BYTES - 2 * rows * features
        ),
    )(
        token_image[None],
        tile_count,
        queries,
        out_grad,
        unnormed_keys[0],
        values[0],
        key_gain[None],
        key_projection_matrix,
        value_projection_matrix,
    )
    return result[None]


def body(*args):
    n_seq, n_img, n_dp = (lax.axis_size(name) for name in ("seq", "img", "dp"))
    rows, width = args[3].shape[1:]
    heads = width // HEAD_WIDTH
    group = args[0].shape[1] // width
    fits = n_img == heads == 2 and n_seq == n_dp == 4 and args[7].shape[1] == width and rows % 8 == 0
    if fits and rows % CHUNK and rows % CHUNK % 16 == 8:
        return body_kernel((n_seq, n_dp, heads, group), *args)
    return body_any(*args)


def solution(mesh):
    in_specs = (
        P("seq", "dp"),
        P("seq", "dp"),
        P("seq"),
        P("img", "seq", "dp"),
        P("img", "seq", "dp"),
        P(),
        P(),
        P("dp", "seq"),
        P("dp", "seq"),
    )
    out_specs = P("img", "seq", "dp")
    return jax.shard_map(body, mesh=mesh, in_specs=in_specs, out_specs=out_specs, check_vma=False)
```
